32 devices in a mesh: ifg: 8 (over y, x, core), row: 4 (over z).
Axes of the slice: x: 2, y: 2, z: 4, core: 2. Of those that a mesh axis runs over, the one named last changes fastest.
Arguments:
- ifg_real: bfloat16 [256, 256, 512], P('ifg', 'row'), may hold values from -6 to 6
- ifg_imag: bfloat16 [256, 256, 512], P('ifg', 'row'), may hold values from -6 to 6
- date_pairs: int32 [256, 2], replicated, may hold values from 0 to 319, as said below
Outputs:
- corrected: float32 [320, 256, 512], P('ifg', 'row')
- atmosphere: float32 [320, 256, 512], P('ifg', 'row')
The draws below stay inside these ranges and needn't reach their ends.
Inputs may be any that keep to these rules, and one draw needn't show every extreme that they name: `date_pairs`: each row holds a reference date and a later secondary date, 1 to 5 dates apart.
All inputs are finite; a program needn't handle non-finite values.
Results may differ from the reference program's by a relative error of at most 0.0078.
Values may be sent and summed in bfloat16 or wider, within the bound.
A program may use at most 128 MiB of HBM per device.

```python
import math
import jax
import jax.numpy as jnp
from jax import lax

COLS = 512
PATCH = 64
NDATES = 320
ITERS = 3
RADIUS = 16
NIFG = 256
ROWS = 256


def draw_date_pairs(key, part):
    key_spacing = jax.random.fold_in(key, 11)
    key_earlier = jax.random.fold_in(key, 12)
    spacing = jax.random.randint(key_spacing, (NIFG,), 1, 6)
    earlier = jax.random.randint(key_earlier, (NIFG,), 0, NDATES - 5)
    position = jnp.arange(NIFG)
    earlier = jnp.where(position == 0, 0, earlier)
    earlier = jnp.where(position == NIFG - 1, NDATES - 1 - spacing, earlier)
    return jnp.stack([earlier, earlier + spacing], axis=1).astype(jnp.int32)


def block_levels(key, shape, cuts, least, top_value):
    factor_of, own = 1.0, jax.random.fold_in(key, 6)
    for dim, blocks in cuts:
        steps = jnp.exp(jax.random.uniform(jax.random.fold_in(own, dim), (blocks,), jnp.float32, least / len(cuts), top_value / len(cuts)))
        factor_of = factor_of * jnp.repeat(steps, shape[dim] // blocks).reshape([-1 if axis == dim else 1 for axis in range(len(shape))])
    return factor_of


def noise(own_key, dims, spread, limit, cuts=(), kind=jnp.bfloat16):
    gain = block_levels(own_key, dims, cuts, -0.22, 0.18) if cuts else 1.0
    array = jax.random.normal(own_key, dims, jnp.float32) * spread * gain
    return jnp.minimum(jnp.maximum(array, -limit), limit).astype(kind)


def setup_inputs(seed: int = 0) -> dict:
    splits = jax.random.split(jax.random.key(seed), 4)
    ifg_real = noise(splits[0], (NIFG, ROWS, COLS), 1.0, 6.0, ((0, 8), (1, 4)))
    ifg_imag = noise(splits[1], (NIFG, ROWS, COLS), 1.0, 6.0, ((0, 8), (1, 4)))
    date_pairs = draw_date_pairs(jax.random.fold_in(splits[3], 71), 0)
    return dict(ifg_real=ifg_real, ifg_imag=ifg_imag, date_pairs=date_pairs)


goldstein_power = 0.5
huber_threshold = 0.3
blur_sigma = 5.0
ridge_weight = 1.0

def spectral_tables():
    counter = jnp.arange(PATCH, dtype=jnp.int32)
    phase_steps = counter[:, None] * counter[None, :] % PATCH
    angles = phase_steps.astype(jnp.float32) * (2.0 * math.pi / PATCH)
    scaling = 1.0 / math.sqrt(PATCH)
    cosine = jnp.cos(angles) * scaling
    sine_lookup = jnp.sin(angles) * scaling
    forward = jnp.concatenate([jnp.concatenate([cosine, -sine_lookup], 1), jnp.concatenate([sine_lookup, cosine], 1)], 0)
    inverse = jnp.concatenate([jnp.concatenate([cosine, sine_lookup], 1), jnp.concatenate([-sine_lookup, cosine], 1)], 0)
    taper_row = jnp.sin(math.pi * (jnp.arange(PATCH, dtype=jnp.float32) + 0.5) / PATCH) ** 2
    return (forward.astype(jnp.bfloat16), inverse.astype(jnp.bfloat16), cosine.astype(jnp.bfloat16), sine_lookup.astype(jnp.bfloat16), taper_row)

def row_apply(values, cosine, sine_lookup, direction):
    flipped = jnp.concatenate([values[..., PATCH:], -values[..., :PATCH]], axis=-1)
    first = jnp.einsum('kb,anbcl->ankcl', cosine.astype(jnp.float32), values.astype(jnp.float32))
    second = jnp.einsum('kb,anbcl->ankcl', sine_lookup.astype(jnp.float32), flipped.astype(jnp.float32))
    return first + direction * second

def filter_block(padded, tables):
    forward, inverse, cosine, sine_lookup, taper_row = tables
    block_count = padded.shape[0]
    rows_pad = padded.shape[2]
    cols_pad = padded.shape[3]
    half_patch = PATCH // 2
    taper_both = jnp.concatenate([taper_row, taper_row])
    canvas = jnp.zeros((block_count, 2, rows_pad, cols_pad), jnp.float32)
    for row_shift in (0, half_patch):
        for col_shift in (0, half_patch):
            window = padded[:, :, row_shift:rows_pad - row_shift, col_shift:cols_pad - col_shift]
            row_tiles = window.shape[2] // PATCH
            col_tiles = window.shape[3] // PATCH
            tile_grid = window.reshape(block_count, 2, row_tiles, PATCH, col_tiles, PATCH)
            stacked = jnp.concatenate([tile_grid[:, 0], tile_grid[:, 1]], axis=-1)
            column_spectra = jnp.einsum('anbcl,lm->anbcm', stacked.astype(jnp.float32), forward.astype(jnp.float32)).astype(jnp.bfloat16)
            spectra = row_apply(column_spectra, cosine, sine_lookup, 1.0)
            spectral_power = spectra[..., :PATCH] ** 2 + spectra[..., PATCH:] ** 2 + 1.0
            shaping = spectral_power ** (0.5 * goldstein_power)
            shaped = (spectra * jnp.concatenate([shaping, shaping], axis=-1)).astype(jnp.bfloat16)
            row_back = row_apply(shaped, cosine, sine_lookup, -1.0).astype(jnp.bfloat16)
            restored = jnp.einsum('anbcl,lm->anbcm', row_back.astype(jnp.float32), inverse.astype(jnp.float32))
            weighted = restored * taper_row[:, None, None] * taper_both
            pieces = jnp.stack([weighted[..., :PATCH], weighted[..., PATCH:]], axis=1)
            pieces = pieces.reshape(block_count, 2, row_tiles * PATCH, col_tiles * PATCH)
            canvas = canvas + jnp.pad(pieces, ((0, 0), (0, 0), (row_shift, row_shift), (col_shift, col_shift)))
    return canvas[:, :, half_patch:rows_pad - half_patch, half_patch:cols_pad - half_patch]

def sine_of(real_part, imag_part):
    real_wide = real_part.astype(jnp.float32)
    imag_wide = imag_part.astype(jnp.float32)
    return (imag_wide / jnp.sqrt(real_wide * real_wide + imag_wide * imag_wide + 1.0)).astype(jnp.bfloat16)

def projection(date_pairs):
    date_index = jnp.arange(NDATES, dtype=jnp.int32)
    design = (date_pairs[:, 1:2] == date_index[None, :]).astype(jnp.float32) - (date_pairs[:, 0:1] == date_index[None, :]).astype(jnp.float32)
    gram = jnp.dot(design.T, design, precision=lax.Precision.HIGHEST) + ridge_weight * jnp.eye(NDATES, dtype=jnp.float32)
    cholesky_factor = jnp.linalg.cholesky(gram)
    halfway = lax.linalg.triangular_solve(cholesky_factor, design.T, left_side=True, lower=True)
    mapping = lax.linalg.triangular_solve(cholesky_factor, halfway, left_side=True, lower=True, transpose_a=True)
    return (design, mapping)

def invert(observed_sines, design, mapping):
    observed = observed_sines.astype(jnp.float32)
    series = jnp.zeros((NDATES, observed.shape[1]), jnp.float32)
    misfit = observed
    for iteration in range(ITERS):
        if iteration > 0:
            misfit = observed - jnp.dot(design, series, precision=lax.Precision.HIGHEST)
        series = series + jnp.dot(mapping, jnp.clip(misfit, -huber_threshold, huber_threshold), precision=lax.Precision.HIGHEST)
    return series

def gauss_matrix(size_out, size_in, offset):
    out_index = jnp.arange(size_out, dtype=jnp.int32)[:, None]
    in_index = jnp.arange(size_in, dtype=jnp.int32)[None, :]
    distance = in_index - offset - out_index
    kernel = jnp.exp(-0.5 * (distance.astype(jnp.float32) / blur_sigma) ** 2)
    return jnp.where(jnp.abs(distance) <= RADIUS, kernel, 0.0)

def reference(ifg_real, ifg_imag, date_pairs):
    tables = spectral_tables()
    half_patch = PATCH // 2
    joined = jnp.stack([ifg_real, ifg_imag], axis=1)
    padded = jnp.pad(joined, ((0, 0), (0, 0), (half_patch, half_patch), (half_patch, half_patch)))
    block_list = padded.reshape(NIFG // 2, 2, 2, ROWS + PATCH, COLS + PATCH)

    def run_block(block_data):
        return filter_block(block_data, tables).astype(jnp.bfloat16)
    filtered = lax.map(run_block, block_list).reshape(NIFG, 2, ROWS, COLS)
    phase_sines = sine_of(filtered[:, 0], filtered[:, 1])
    design, mapping = projection(date_pairs)
    series = invert(phase_sines.reshape(NIFG, ROWS * COLS), design, mapping).reshape(NDATES, ROWS, COLS)
    col_kernel = gauss_matrix(COLS, COLS, 0)
    row_filter_kernel = gauss_matrix(ROWS, ROWS, 0)
    smoothed_columns = jnp.einsum('drc,ce->dre', series, col_kernel, precision=lax.Precision.HIGHEST)
    smoothed_phase = jnp.einsum('om,nmb->nob', row_filter_kernel, smoothed_columns, precision=lax.Precision.HIGHEST)
    weight = lax.optimization_barrier(jnp.sum(row_filter_kernel, axis=1))[:, None] * lax.optimization_barrier(jnp.sum(col_kernel, axis=0))[None, :]
    atmosphere = smoothed_phase / weight
    return (series - atmosphere, atmosphere)
```

```python
import functools
import math

import jax
import jax.numpy as jnp
import numpy as np
from jax import lax
from jax.experimental import pallas as pl
from jax.experimental.pallas import tpu as pltpu
from jax.sharding import PartitionSpec as P

PATCH = 64
HALF = PATCH // 2
RADIUS = 16
NDATES = 320
ITERS = 3

huber_threshold = 0.3
blur_sigma = 5.0

BF = jnp.bfloat16
F32 = jnp.float32
CHUNKS = 2


def mm(a, b):
    return jnp.dot(a, b, preferred_element_type=F32)


def split2(x):
    high = x.astype(BF)
    return high, (x - high.astype(F32)).astype(BF)


def split3(x):
    high = x.astype(BF)
    rest = x - high.astype(F32)
    mid = rest.astype(BF)
    return high, mid, (rest - mid.astype(F32)).astype(BF)


def mm3(a, b):
    ah, al = split2(a)
    bh, bl = split2(b)
    return mm(ah, bh) + (mm(ah, bl) + mm(al, bh))


def spectral_tables(local_rows):
    k = np.arange(PATCH)
    angles = ((k[:, None] * k[None, :]) % PATCH).astype(np.float32) * np.float32(
        2.0 * math.pi / PATCH
    )
    scaling = np.float32(1.0 / math.sqrt(PATCH))
    rounded = lambda v: np.asarray(v.astype(np.float32)).astype(BF).astype(np.float32)
    c = rounded(np.cos(angles) * scaling)
    s = rounded(np.sin(angles) * scaling)
    taper = (
        np.sin(np.float32(math.pi) * (k.astype(np.float32) + np.float32(0.5)) / PATCH) ** 2
    ).astype(np.float32)
    two = np.eye(2, dtype=np.float32)
    cc, ss = np.kron(two, c), np.kron(two, s)
    col_forward = np.block([[cc, -ss], [ss, cc]])
    col_inverse = np.block([[cc, ss], [-ss, cc]])
    extended = local_rows + PATCH
    starts = list(range(0, extended - PATCH + 1, HALF))
    count = len(starts)
    row_forward = np.zeros((2, count, PATCH, 2, extended), np.float32)
    row_inverse = np.zeros((2, extended, 2, count, PATCH), np.float32)
    for p, at in enumerate(starts):
        where = slice(at, at + PATCH)
        row_forward[0, p, :, 0, where] = c
        row_forward[0, p, :, 1, where] = s
        row_forward[1, p, :, 0, where] = -s
        row_forward[1, p, :, 1, where] = c
        tc, ts = taper[:, None] * c, taper[:, None] * s
        row_inverse[0, where, 0, p, :] = tc
        row_inverse[0, where, 1, p, :] = -ts
        row_inverse[1, where, 0, p, :] = ts
        row_inverse[1, where, 1, p, :] = tc
    row_forward = row_forward.reshape(2 * count * PATCH, 2 * extended)
    row_inverse = row_inverse[:, HALF : HALF + local_rows].reshape(
        2 * local_rows, 2 * count * PATCH
    )
    return (
        jnp.asarray(col_forward.astype(BF)),
        jnp.asarray(row_forward.astype(BF)),
        jnp.asarray(row_inverse.astype(BF)),
        jnp.asarray(col_inverse.astype(BF)),
        jnp.asarray(np.tile(taper, 4)[None, :]),
    )


def filter_kernel(re, im, low_re, low_im, high_re, high_im, cf, rf, ri, ci, tp, out, *scratch):
    pad_re, pad_im, even_re, even_im, odd_re, odd_im = scratch
    group, rows, cols = re.shape
    extended = rows + PATCH
    wide = pad_re.shape[1]
    even_tiles = cols // 128
    odd_tiles = wide // 128
    tiles = even_tiles + odd_tiles
    half = rf.shape[0] // 2

    @pl.when(pl.program_id(0) == 0)
    def _():
        pad_re[...] = jnp.zeros_like(pad_re)
        pad_im[...] = jnp.zeros_like(pad_im)

    def one(i, carry):
        x_re = jnp.concatenate([low_re[i], re[i], high_re[i]], axis=0)
        x_im = jnp.concatenate([low_im[i], im[i], high_im[i]], axis=0)
        pad_re[:, HALF : HALF + cols] = x_re
        pad_im[:, HALF : HALF + cols] = x_im

        def tile_of(t):
            if t < even_tiles:
                at = slice(128 * t, 128 * t + 128)
                return jnp.concatenate([x_re[:, at], x_im[:, at]], axis=1)
            at = slice(128 * (t - even_tiles), 128 * (t - even_tiles) + 128)
            return jnp.concatenate([pad_re[:, at], pad_im[:, at]], axis=1)

        for first in range(0, tiles, 2):
            members = list(range(first, min(first + 2, tiles)))
            stacked = jnp.concatenate([tile_of(t) for t in members], axis=0)
            y = mm(stacked, cf[...]).astype(BF)
            parts = []
            for n in range(len(members)):
                piece = y[n * extended : (n + 1) * extended]
                parts.append(jnp.concatenate([piece[:, :128], piece[:, 128:]], axis=0))
            z = mm(rf[...], jnp.concatenate(parts, axis=1))
            z_re, z_im = z[:half], z[half:]
            gain = lax.rsqrt(lax.rsqrt(z_re * z_re + z_im * z_im + 1.0))
            q = jnp.concatenate([(z_re * gain).astype(BF), (z_im * gain).astype(BF)], axis=0)
            u = mm(ri[...], q).astype(BF)
            parts = []
            for n in range(len(members)):
                at = slice(128 * n, 128 * n + 128)
                parts.append(jnp.concatenate([u[:rows, at], u[rows:, at]], axis=1))
            v = mm(jnp.concatenate(parts, axis=0), ci[...]) * tp[...]
            for n, t in enumerate(members):
                piece = v[n * rows : (n + 1) * rows]
                if t < even_tiles:
                    at = slice(128 * t, 128 * t + 128)
                    even_re[:, at] = piece[:, :128]
                    even_im[:, at] = piece[:, 128:]
                else:
                    at = slice(128 * (t - even_tiles), 128 * (t - even_tiles) + 128)
                    odd_re[:, at] = piece[:, :128]
                    odd_im[:, at] = piece[:, 128:]
        f_re = even_re[...] + odd_re[:, HALF : HALF + cols]
        f_im = even_im[...] + odd_im[:, HALF : HALF + cols]
        out[i] = (f_im * lax.rsqrt(f_re * f_re + f_im * f_im + 1.0)).astype(BF)
        return carry

    lax.fori_loop(0, group, one, 0)


def filtered_sines(re, im, halos, tables):
    count, rows, cols = re.shape
    group = 8 if count % 8 == 0 else count
    wide = -(-(cols + PATCH) // 128) * 128
    extended = rows + PATCH
    whole = pl.BlockSpec((group, rows, cols), lambda i: (i, 0, 0))
    part = pl.BlockSpec((group, HALF, cols), lambda i: (i, 0, 0))
    fixed = [pl.BlockSpec(t.shape, lambda i: (0, 0)) for t in tables]
    flops = 2 * count * 9 * (extended + 5 * rows) * 65536
    return pl.pallas_call(
        filter_kernel,
        grid=(count // group,),
        in_specs=[whole, whole, part, part, part, part] + fixed,
        out_specs=whole,
        out_shape=jax.ShapeDtypeStruct((count, rows, cols), BF),
        scratch_shapes=[
            pltpu.VMEM((extended, wide), BF),
            pltpu.VMEM((extended, wide), BF),
            pltpu.VMEM((rows, cols), F32),
            pltpu.VMEM((rows, cols), F32),
            pltpu.VMEM((rows, wide), F32),
            pltpu.VMEM((rows, wide), F32),
        ],
        compiler_params=pltpu.CompilerParams(vmem_limit_bytes=40 << 20),
        cost_estimate=pl.CostEstimate(
            flops=flops, bytes_accessed=count * rows * cols * 8, transcendentals=0
        ),
        name="goldstein",
    )(re, im, *halos, *tables)


def inverse_kernel(steps, pairs, pairs_t, k_hi, k_lo, p_hi, p_lo):
    n = pairs.shape[0]
    dates = p_hi.shape[0]
    a, b = pairs[:, 0:1], pairs[:, 1:2]
    at, bt = pairs_t[0:1, :], pairs_t[1:2, :]
    one = lambda m: jnp.where(m, 1.0, 0.0)
    row = lax.broadcasted_iota(jnp.int32, (n, n), 0)
    col = lax.broadcasted_iota(jnp.int32, (n, n), 1)
    eye = one(row == col)
    matrix = one(a == at) + one(b == bt) - one(a == bt) - one(b == at) + eye
    exact = matrix.astype(BF)
    top = jnp.max(jnp.sum(jnp.abs(matrix), axis=1, keepdims=True), axis=0, keepdims=True)
    rho = (top - 1.0) / (top + 1.0)
    x = eye * (2.0 / (top + 1.0))

    def refine(_, carry):
        x, rho = carry
        xh, xm, xl = split3(x)
        residual = eye - (mm(exact, xh) + (mm(exact, xm) + mm(exact, xl)))
        scale = 2.0 / (2.0 - rho * rho)
        return (x + mm3(x, residual)) * scale, rho * rho / (2.0 - rho * rho)

    x, rho = lax.fori_loop(0, steps, refine, (x, rho))
    xh, xm, xl = split3(x)
    date = lax.broadcasted_iota(jnp.int32, (dates, n), 0)
    design_t = (one(date == bt) - one(date == at)).astype(BF)
    k_hi[...], k_lo[...] = split2(x)
    p_hi[...], p_lo[...] = split2(mm(design_t, xh) + (mm(design_t, xm) + mm(design_t, xl)))


def inverse_tables(date_pairs):
    n = date_pairs.shape[0]
    top, steps = 2.0 * n + 1.0, 0
    rho = (top - 1.0) / (top + 1.0)
    while rho > 1e-7:
        rho = rho * rho / (2.0 - rho * rho)
        steps += 1
    vmem = pl.BlockSpec(memory_space=pltpu.VMEM)
    return pl.pallas_call(
        functools.partial(inverse_kernel, steps),
        in_specs=[vmem, vmem],
        out_specs=[vmem] * 4,
        out_shape=[jax.ShapeDtypeStruct((n, n), BF)] * 2
        + [jax.ShapeDtypeStruct((NDATES, n), BF)] * 2,
        compiler_params=pltpu.CompilerParams(vmem_limit_bytes=40 << 20),
        cost_estimate=pl.CostEstimate(
            flops=steps * 6 * 4 * n**3, bytes_accessed=8 * n * n, transcendentals=0
        ),
        name="newton",
    )(date_pairs, date_pairs.T)


def invert_kernel(d_ref, k_hi, k_lo, p_hi, p_lo, out):
    d = d_ref[0].astype(F32)
    clip = lambda r: jnp.minimum(jnp.maximum(r, -huber_threshold), huber_threshold)

    def apply(high, low, v):
        vh, vl = split2(v)
        return mm(high[...], vh) + (mm(low[...], vh) + mm(high[...], vl))

    total = clip(d)
    for _ in range(ITERS - 1):
        total = total + clip(d - total + apply(k_hi, k_lo, total))
    out[0] = apply(p_hi, p_lo, total).astype(out.dtype)


def invert(sines, tables):
    strips, n, cols = sines.shape
    fixed = [pl.BlockSpec(t.shape, lambda i: (0, 0)) for t in tables]
    return pl.pallas_call(
        invert_kernel,
        grid=(strips,),
        in_specs=[pl.BlockSpec((1, n, cols), lambda i: (i, 0, 0))] + fixed,
        out_specs=pl.BlockSpec((1, NDATES, cols), lambda i: (i, 0, 0)),
        out_shape=jax.ShapeDtypeStruct((strips, NDATES, cols), BF),
        compiler_params=pltpu.CompilerParams(vmem_limit_bytes=40 << 20),
        name="huber",
    )(sines, *tables)


def gauss_matrix(size_out, size_in, offset):
    distance = np.arange(size_in)[None, :] - offset - np.arange(size_out)[:, None]
    kernel = np.exp(-0.5 * (distance.astype(np.float32) / np.float32(blur_sigma)) ** 2)
    return np.where(np.abs(distance) <= RADIUS, kernel, 0.0).astype(np.float32)


def blur_kernel(own, low, high, rk, ck_hi, ck_lo, inv_row, inv_col, corrected, atmosphere):
    group, rows, cols = own.shape
    pieces = []
    for i in range(group):
        extended = jnp.concatenate([low[i], own[i], high[i]], axis=0)
        both = mm(rk[...], extended)
        pieces.append((both[:rows] + both[rows:]).astype(BF))
    stacked = jnp.concatenate(pieces, axis=0)
    smooth = mm(stacked, ck_hi[...]) + mm(stacked, ck_lo[...])
    for i in range(group):
        air = smooth[i * rows : (i + 1) * rows] * inv_row[...] * inv_col[...]
        atmosphere[i] = air
        corrected[i] = own[i].astype(F32) - air


def blur(own, low, high):
    dates, rows, cols = own.shape
    group = next(g for g in (8, 5, 4, 2, 1) if dates % g == 0)
    hi = lambda v: v.astype(BF)
    lo = lambda v: (v - v.astype(BF).astype(np.float32)).astype(BF)
    row_filter = gauss_matrix(rows, rows + 2 * RADIUS, RADIUS)
    col_filter = gauss_matrix(cols, cols, 0)
    row_tables = jnp.asarray(np.concatenate([hi(row_filter), lo(row_filter)], axis=0))
    source = lax.axis_index("row") * rows - RADIUS + jnp.arange(rows + 2 * RADIUS, dtype=jnp.int32)
    inside = (source >= 0) & (source < rows * lax.axis_size("row"))
    row_weight = jnp.sum(jnp.where(inside[None, :], jnp.asarray(row_filter), 0.0), axis=1)
    fixed = [
        row_tables,
        jnp.asarray(hi(col_filter)),
        jnp.asarray(lo(col_filter)),
        (1.0 / row_weight)[:, None],
        jnp.asarray(1.0 / col_filter.sum(axis=0, dtype=np.float32))[None, :],
    ]
    block = pl.BlockSpec((group, rows, cols), lambda i: (i, 0, 0))
    edge = pl.BlockSpec((group, RADIUS, cols), lambda i: (i, 0, 0))
    return pl.pallas_call(
        blur_kernel,
        grid=(dates // group,),
        in_specs=[block, edge, edge] + [pl.BlockSpec(t.shape, lambda i: (0, 0)) for t in fixed],
        out_specs=[block, block],
        out_shape=[jax.ShapeDtypeStruct((dates, rows, cols), F32)] * 2,
        compiler_params=pltpu.CompilerParams(vmem_limit_bytes=50 << 20),
        name="blur",
    )(own, low, high, *fixed)


def from_neighbours(block, axis, dim, width):
    count = lax.axis_size(axis)
    forward = [(i, i + 1) for i in range(count - 1)]
    backward = [(target, source) for source, target in forward]
    low = lax.ppermute(
        lax.slice_in_dim(block, block.shape[dim] - width, None, axis=dim), axis, forward
    )
    high = lax.ppermute(lax.slice_in_dim(block, 0, width, axis=dim), axis, backward)
    return low, high


def on_device(ifg_real, ifg_imag, date_pairs):
    count, rows, cols = ifg_real.shape
    parts = lax.axis_size("ifg")
    chunks = CHUNKS if count % (8 * CHUNKS) == 0 else 1
    size = count // chunks
    strip = rows // parts
    tables = spectral_tables(rows)
    halos = []
    for n in range(chunks):
        at = slice(n * size, (n + 1) * size)
        low_re, high_re = from_neighbours(ifg_real[at], "row", 1, HALF)
        low_im, high_im = from_neighbours(ifg_imag[at], "row", 1, HALF)
        halos.append((low_re, low_im, high_re, high_im))
    solver = inverse_tables(date_pairs)
    arrived = []
    for n in range(chunks):
        at = slice(n * size, (n + 1) * size)
        sines = filtered_sines(ifg_real[at], ifg_imag[at], halos[n], tables)
        sines = sines.reshape(size, parts, strip, cols).transpose(1, 2, 0, 3)
        arrived.append(lax.all_to_all(sines, "ifg", split_axis=0, concat_axis=0, tiled=True))
    sines = jnp.stack(arrived)
    sines = sines.transpose(2, 1, 0, 3, 4).reshape(strip, parts * count, cols)
    series = invert(sines, solver)
    mine = NDATES // parts
    series = series.reshape(strip, parts, mine, cols).transpose(1, 2, 0, 3)
    values = lax.all_to_all(series, "ifg", split_axis=0, concat_axis=0, tiled=True)
    values = values.transpose(1, 0, 2, 3).reshape(mine, rows, cols)
    low, high = from_neighbours(values, "row", 1, RADIUS)
    return tuple(blur(values, low, high))


def solution(mesh):
    placed = (P("ifg", "row", None), P("ifg", "row", None), P())
    return jax.shard_map(
        on_device,
        mesh=mesh,
        in_specs=placed,
        out_specs=(P("ifg", "row", None), P("ifg", "row", None)),
        check_vma=False,
    )
```

```python
import functools
import math

import jax
import jax.numpy as jnp
import numpy as np
from jax import lax
from jax.experimental import pallas as pl
from jax.experimental.pallas import tpu as pltpu
from jax.sharding import PartitionSpec as P

PATCH = 64
HALF = PATCH // 2
RADIUS = 16
NDATES = 320
ITERS = 3

huber_threshold = 0.3
blur_sigma = 5.0

BF = jnp.bfloat16
F32 = jnp.float32


def mm(a, b):
    return jnp.dot(a, b, preferred_element_type=F32)


def split2(x):
    high = x.astype(BF)
    return high, (x - high.astype(F32)).astype(BF)


def split3(x):
    high = x.astype(BF)
    rest = x - high.astype(F32)
    mid = rest.astype(BF)
    return high, mid, (rest - mid.astype(F32)).astype(BF)


def mm3(a, b):
    ah, al = split2(a)
    bh, bl = split2(b)
    return mm(ah, bh) + (mm(ah, bl) + mm(al, bh))


def spectral_tables(local_rows):
    k = np.arange(PATCH)
    angles = ((k[:, None] * k[None, :]) % PATCH).astype(np.float32) * np.float32(
        2.0 * math.pi / PATCH
    )
    scaling = np.float32(1.0 / math.sqrt(PATCH))
    rounded = lambda v: np.asarray(v.astype(np.float32)).astype(BF).astype(np.float32)
    c = rounded(np.cos(angles) * scaling)
    s = rounded(np.sin(angles) * scaling)
    taper = (
        np.sin(np.float32(math.pi) * (k.astype(np.float32) + np.float32(0.5)) / PATCH) ** 2
    ).astype(np.float32)
    two = np.eye(2, dtype=np.float32)
    cc, ss = np.kron(two, c), np.kron(two, s)
    col_forward = np.block([[cc, -ss], [ss, cc]])
    col_inverse = np.block([[cc, ss], [-ss, cc]])
    extended = local_rows + PATCH
    starts = list(range(0, extended - PATCH + 1, HALF))
    count = len(starts)
    row_forward = np.zeros((2, count, PATCH, 2, extended), np.float32)
    row_inverse = np.zeros((2, extended, 2, count, PATCH), np.float32)
    for p, at in enumerate(starts):
        where = slice(at, at + PATCH)
        row_forward[0, p, :, 0, where] = c
        row_forward[0, p, :, 1, where] = s
        row_forward[1, p, :, 0, where] = -s
        row_forward[1, p, :, 1, where] = c
        tc, ts = taper[:, None] * c, taper[:, None] * s
        row_inverse[0, where, 0, p, :] = tc
        row_inverse[0, where, 1, p, :] = -ts
        row_inverse[1, where, 0, p, :] = ts
        row_inverse[1, where, 1, p, :] = tc
    row_forward = row_forward.reshape(2 * count * PATCH, 2 * extended)
    row_inverse = row_inverse[:, HALF : HALF + local_rows].reshape(
        2 * local_rows, 2 * count * PATCH
    )
    return (
        jnp.asarray(col_forward.astype(BF)),
        jnp.asarray(row_forward.astype(BF)),
        jnp.asarray(row_inverse.astype(BF)),
        jnp.asarray(col_inverse.astype(BF)),
        jnp.asarray(np.tile(taper, 4)[None, :]),
    )


def pick(sel, first, second, swapped_at, kept_at):
    zero = jnp.zeros_like(first)
    return jnp.where(sel[swapped_at] > 0, first, jnp.where(sel[kept_at] > 0, second, zero))


def filter_kernel(first, width, split, sel, re, im, one, two, *refs):
    if split:
        one_more, two_more, *refs = refs
    cf, rf, ri, ci, tp, out, pad_re, pad_im, even_re, even_im, odd_re, odd_im = refs
    group, rows, cols = re.shape
    extended = rows + PATCH
    window = width + 128
    start = 128 * first
    per = width // 128
    tiles = [(True, t) for t in range(per)] + [(False, t) for t in range(per + 1)]
    half = rf.shape[0] // 2

    @pl.when(pl.program_id(0) == 0)
    def _():
        pad_re[...] = jnp.zeros_like(pad_re)
        pad_im[...] = jnp.zeros_like(pad_im)

    def halo(part, i):
        p, q = one[part, i], two[part, i]
        if split:
            p = jnp.concatenate([p[:, start:], one_more[part, i]], axis=1)
            q = jnp.concatenate([q[:, start:], two_more[part, i]], axis=1)
        return pick(sel, p, q, 0, 1), pick(sel, p, q, 2, 3)

    def load(i, slot):
        made = []
        for part, own, pad in ((0, re, pad_re), (1, im, pad_im)):
            low, high = halo(part, i)
            x = jnp.concatenate([low, own[i, :, start : start + window], high], axis=0)
            pad[slot, :, HALF : HALF + window] = x
            made.append(x)
        return made

    def pair(step, carry):
        images = [load(2 * step + slot, slot) for slot in range(2)]
        members = [(slot, *tile) for tile in tiles for slot in range(2)]
        blocks = [members[n : n + 2] for n in range(0, len(members), 2)]

        def tile_of(slot, even, t):
            at = slice(start + 128 * t, start + 128 * t + 128)
            if even:
                return jnp.concatenate([x[:, at] for x in images[slot]], axis=1)
            return jnp.concatenate([pad_re[slot, :, at], pad_im[slot, :, at]], axis=1)

        def columns(n):
            stacked = jnp.concatenate([tile_of(*m) for m in blocks[n]], axis=0)
            y = mm(stacked, cf[...]).astype(BF)
            return jnp.concatenate(
                [
                    jnp.concatenate([y[:extended, :128], y[:extended, 128:]], axis=0),
                    jnp.concatenate([y[extended:, :128], y[extended:, 128:]], axis=0),
                ],
                axis=1,
            )

        def spectrum(y):
            z = mm(rf[...], y)
            z_re, z_im = z[:half], z[half:]
            gain = lax.rsqrt(lax.rsqrt(z_re * z_re + z_im * z_im + 1.0))
            return jnp.concatenate([(z_re * gain).astype(BF), (z_im * gain).astype(BF)], axis=0)

        def rows_back(q):
            u = mm(ri[...], q).astype(BF)
            return jnp.concatenate(
                [
                    jnp.concatenate([u[:rows, :128], u[rows:, :128]], axis=1),
                    jnp.concatenate([u[:rows, 128:], u[rows:, 128:]], axis=1),
                ],
                axis=0,
            )

        def columns_back(n, u):
            v = mm(u, ci[...]) * tp[...]
            for m, (slot, even, t) in enumerate(blocks[n]):
                piece = v[m * rows : (m + 1) * rows]
                at = slice(128 * t, 128 * t + 128)
                (even_re if even else odd_re)[slot, :, at] = piece[:, :128]
                (even_im if even else odd_im)[slot, :, at] = piece[:, 128:]

        count = len(blocks)
        y, q, u = {}, {}, {}
        for tick in range(count + 3):
            if tick < count:
                y[tick] = columns(tick)
            if 0 <= tick - 1 < count:
                q[tick - 1] = spectrum(y.pop(tick - 1))
            if 0 <= tick - 2 < count:
                u[tick - 2] = rows_back(q.pop(tick - 2))
            if 0 <= tick - 3 < count:
                columns_back(tick - 3, u.pop(tick - 3))
        for slot in range(2):
            f_re = even_re[slot] + odd_re[slot, :, HALF : HALF + width]
            f_im = even_im[slot] + odd_im[slot, :, HALF : HALF + width]
            out[2 * step + slot] = (f_im * lax.rsqrt(f_re * f_re + f_im * f_im + 1.0)).astype(BF)
        return carry

    lax.fori_loop(0, group // 2, pair, 0)


def filtered_sines(re, im, sel, halos, more, tables, at, count, first, width):
    rows, cols = re.shape[1:]
    group = 8
    extended = rows + PATCH
    skip = at // group
    whole = pl.BlockSpec((group, rows, cols), lambda i: (i + skip, 0, 0))
    edge = pl.BlockSpec((2, group, HALF, width + 128), lambda i: (0, i, 0, 0))
    rest = pl.BlockSpec((2, group, HALF, cols - width - 128), lambda i: (0, i + skip, 0, 0))
    fixed = [pl.BlockSpec(t.shape, lambda i: (0, 0)) for t in tables]
    return pl.pallas_call(
        functools.partial(filter_kernel, first, width, bool(more)),
        grid=(count // group,),
        in_specs=[pl.BlockSpec(memory_space=pltpu.SMEM), whole, whole, edge, edge]
        + [rest] * len(more)
        + fixed,
        out_specs=pl.BlockSpec((group, rows, width), lambda i: (i, 0, 0)),
        out_shape=jax.ShapeDtypeStruct((count, rows, width), BF),
        scratch_shapes=[pltpu.VMEM((2, extended, width + 256), BF)] * 2
        + [pltpu.VMEM((2, rows, width), F32)] * 2
        + [pltpu.VMEM((2, rows, width + 128), F32)] * 2,
        compiler_params=pltpu.CompilerParams(vmem_limit_bytes=32 << 20),
        cost_estimate=pl.CostEstimate(
            flops=count * width * 3000000, bytes_accessed=count * rows * cols * 4, transcendentals=0
        ),
        name="goldstein",
    )(sel, re, im, *halos, *more, *tables)


def inverse_kernel(steps, pairs, pairs_t, k_hi, k_lo, p_hi, p_lo):
    n = pairs.shape[0]
    dates = p_hi.shape[0]
    a, b = pairs[:, 0:1], pairs[:, 1:2]
    at, bt = pairs_t[0:1, :], pairs_t[1:2, :]
    one = lambda m: jnp.where(m, 1.0, 0.0)
    row = lax.broadcasted_iota(jnp.int32, (n, n), 0)
    col = lax.broadcasted_iota(jnp.int32, (n, n), 1)
    eye = one(row == col)
    matrix = one(a == at) + one(b == bt) - one(a == bt) - one(b == at) + eye
    exact = matrix.astype(BF)
    top = jnp.max(jnp.sum(jnp.abs(matrix), axis=1, keepdims=True), axis=0, keepdims=True)
    rho = (top - 1.0) / (top + 1.0)
    x = eye * (2.0 / (top + 1.0))

    def refine(_, carry):
        x, rho = carry
        xh, xm, xl = split3(x)
        residual = eye - (mm(exact, xh) + (mm(exact, xm) + mm(exact, xl)))
        scale = 2.0 / (2.0 - rho * rho)
        return (x + mm3(x, residual)) * scale, rho * rho / (2.0 - rho * rho)

    x, rho = lax.fori_loop(0, steps, refine, (x, rho))
    xh, xm, xl = split3(x)
    date = lax.broadcasted_iota(jnp.int32, (dates, n), 0)
    design_t = (one(date == bt) - one(date == at)).astype(BF)
    k_hi[...], k_lo[...] = split2(x)
    p_hi[...], p_lo[...] = split2(mm(design_t, xh) + (mm(design_t, xm) + mm(design_t, xl)))


def inverse_tables(date_pairs):
    n = date_pairs.shape[0]
    top, steps = 2.0 * n + 1.0, 0
    rho = (top - 1.0) / (top + 1.0)
    while rho > 1e-7:
        rho = rho * rho / (2.0 - rho * rho)
        steps += 1
    vmem = pl.BlockSpec(memory_space=pltpu.VMEM)
    return pl.pallas_call(
        functools.partial(inverse_kernel, steps),
        in_specs=[vmem, vmem],
        out_specs=[vmem] * 4,
        out_shape=[jax.ShapeDtypeStruct((n, n), BF)] * 2
        + [jax.ShapeDtypeStruct((NDATES, n), BF)] * 2,
        compiler_params=pltpu.CompilerParams(vmem_limit_bytes=40 << 20),
        cost_estimate=pl.CostEstimate(
            flops=steps * 6 * 4 * n**3, bytes_accessed=8 * n * n, transcendentals=0
        ),
        name="newton",
    )(date_pairs, date_pairs.T)


def invert_kernel(d_ref, k_hi, k_lo, p_hi, p_lo, out):
    parts, _, held, cols = d_ref.shape
    d = d_ref[:, 0].reshape(parts * held, cols).astype(F32)
    clip = lambda r: jnp.minimum(jnp.maximum(r, -huber_threshold), huber_threshold)

    def apply(high, low, v):
        vh, vl = split2(v)
        return mm(high[...], vh) + (mm(low[...], vh) + mm(high[...], vl))

    total = clip(d)
    for _ in range(ITERS - 1):
        total = total + clip(d - total + apply(k_hi, k_lo, total))
    series = apply(p_hi, p_lo, total)
    out[:, 0] = series.reshape(parts, series.shape[0] // parts, cols).astype(out.dtype)


def invert(sines, tables):
    parts, strips, held, cols = sines.shape
    mine = NDATES // parts
    fixed = [pl.BlockSpec(t.shape, lambda i: (0, 0)) for t in tables]
    n = parts * held
    return pl.pallas_call(
        invert_kernel,
        grid=(strips,),
        in_specs=[pl.BlockSpec((parts, 1, held, cols), lambda i: (0, i, 0, 0))] + fixed,
        out_specs=pl.BlockSpec((parts, 1, mine, cols), lambda i: (0, i, 0, 0)),
        out_shape=jax.ShapeDtypeStruct((parts, strips, mine, cols), BF),
        compiler_params=pltpu.CompilerParams(vmem_limit_bytes=32 << 20),
        cost_estimate=pl.CostEstimate(
            flops=6 * strips * cols * n * (2 * n + NDATES),
            bytes_accessed=4 * strips * cols * n,
            transcendentals=0,
        ),
        name="huber",
    )(sines, *tables)


def gauss_matrix(size_out, size_in, offset):
    distance = np.arange(size_in)[None, :] - offset - np.arange(size_out)[:, None]
    kernel = np.exp(-0.5 * (distance.astype(np.float32) / np.float32(blur_sigma)) ** 2)
    return np.where(np.abs(distance) <= RADIUS, kernel, 0.0).astype(np.float32)


def blur_kernel(halves, sel, *refs):
    owns, ones, twos = refs[:halves], refs[halves : 2 * halves], refs[2 * halves : 3 * halves]
    rk, ck_hi, ck_lo, inv_row, inv_col, corrected, atmosphere = refs[3 * halves :]
    group, rows, cols = corrected.shape
    pieces = []
    own = []
    for i in range(group):
        own.append(jnp.concatenate([o[i] for o in owns], axis=1))
        one = jnp.concatenate([o[i] for o in ones], axis=1)
        two = jnp.concatenate([o[i] for o in twos], axis=1)
        extended = jnp.concatenate(
            [pick(sel, one, two, 0, 1), own[i], pick(sel, one, two, 2, 3)], axis=0
        )
        both = mm(rk[...], extended)
        pieces.append((both[:rows] + both[rows:]).astype(BF))
    stacked = jnp.concatenate(pieces, axis=0)
    smooth = mm(stacked, ck_hi[...]) + mm(stacked, ck_lo[...])
    for i in range(group):
        air = smooth[i * rows : (i + 1) * rows] * inv_row[...] * inv_col[...]
        atmosphere[i] = air
        corrected[i] = own[i].astype(F32) - air


def blur(sel, owns, ones, twos):
    dates, rows, _ = owns[0].shape
    cols = sum(o.shape[2] for o in owns)
    halves = len(owns)
    group = next(g for g in (8, 5, 4, 2, 1) if dates % g == 0)
    hi = lambda v: v.astype(BF)
    lo = lambda v: (v - v.astype(BF).astype(np.float32)).astype(BF)
    row_filter = gauss_matrix(rows, rows + 2 * RADIUS, RADIUS)
    col_filter = gauss_matrix(cols, cols, 0)
    row_tables = jnp.asarray(np.concatenate([hi(row_filter), lo(row_filter)], axis=0))
    source = lax.axis_index("row") * rows - RADIUS + jnp.arange(rows + 2 * RADIUS, dtype=jnp.int32)
    inside = (source >= 0) & (source < rows * lax.axis_size("row"))
    row_weight = jnp.sum(jnp.where(inside[None, :], jnp.asarray(row_filter), 0.0), axis=1)
    fixed = [
        row_tables,
        jnp.asarray(hi(col_filter)),
        jnp.asarray(lo(col_filter)),
        (1.0 / row_weight)[:, None],
        jnp.asarray(1.0 / col_filter.sum(axis=0, dtype=np.float32))[None, :],
    ]
    block = pl.BlockSpec((group, rows, cols), lambda i: (i, 0, 0))
    cut = lambda v: pl.BlockSpec((group,) + v.shape[1:], lambda i: (i, 0, 0))
    arrays = [*owns, *ones, *twos]
    return pl.pallas_call(
        functools.partial(blur_kernel, halves),
        grid=(dates // group,),
        in_specs=[pl.BlockSpec(memory_space=pltpu.SMEM)]
        + [cut(v) for v in arrays]
        + [pl.BlockSpec(t.shape, lambda i: (0, 0)) for t in fixed],
        out_specs=[block, block],
        out_shape=[jax.ShapeDtypeStruct((dates, rows, cols), F32)] * 2,
        compiler_params=pltpu.CompilerParams(vmem_limit_bytes=50 << 20),
        name="blur",
    )(sel, *arrays, *fixed)


def exchange(top, bottom):
    n = lax.axis_size("row")
    even = lax.axis_index("row") % 2 == 0
    received = []
    for first, mine in ((0, jnp.where(even, bottom, top)), (1, jnp.where(even, top, bottom))):
        partner = list(range(n))
        for i in range(first, n - 1, 2):
            partner[i], partner[i + 1] = i + 1, i
        received.append(lax.ppermute(mine, "row", list(enumerate(partner))))
    return received


def sources():
    n, at = lax.axis_size("row"), lax.axis_index("row")
    even = at % 2 == 0
    flags = [~even, even & (at > 0), even & (at < n - 1), ~even & (at < n - 1)]
    return jnp.stack(flags).astype(jnp.int32)


def on_device(ifg_real, ifg_imag, date_pairs):
    count, rows, cols = ifg_real.shape
    parts = lax.axis_size("ifg")
    strip = rows // parts
    width = cols // 2
    cut = width + 128
    tables = spectral_tables(rows)
    groups = [(0, 8), (8, count - 8)] if count > 8 else [(0, count)]
    halos = []
    for at, size in groups:
        joined = jnp.stack([v[at : at + size, :, :cut] for v in (ifg_real, ifg_imag)])
        halos.append(exchange(joined[:, :, :HALF], joined[:, :, rows - HALF :]))
    joined = jnp.stack([v[:, :, cut:] for v in (ifg_real, ifg_imag)])
    more = exchange(joined[:, :, :HALF], joined[:, :, rows - HALF :])
    sel = sources()
    solver = inverse_tables(date_pairs)
    gate, *solver = lax.optimization_barrier((sel, *solver))

    def sines_of(n, gate, first, extra):
        at, size = groups[n]
        return filtered_sines(
            ifg_real, ifg_imag, gate, halos[n], extra, tables, at, size, first, width
        )

    def send(pieces):
        sines = jnp.concatenate(pieces, axis=0) if len(pieces) > 1 else pieces[0]
        sines = sines.reshape(count, parts, strip, width).transpose(1, 2, 0, 3)
        return lax.all_to_all(sines, "ifg", split_axis=0, concat_axis=0, tiled=True)

    def give(series):
        values = lax.all_to_all(series, "ifg", split_axis=0, concat_axis=0, tiled=True)
        values = values.transpose(2, 0, 1, 3).reshape(NDATES // parts, rows, width)
        one, two = exchange(values[:, :RADIUS], values[:, rows - RADIUS :])
        return values, one, two

    skipped = width // 128 - 1
    left = send([sines_of(n, gate, 0, ()) for n in range(len(groups))])
    right = [sines_of(0, gate, skipped, more)]
    series = invert(left, solver)
    gate, series = lax.optimization_barrier((gate, series))
    halves = [give(series)]
    right += [sines_of(n, gate, skipped, more) for n in range(1, len(groups))]
    halves.append(give(invert(send(right), solver)))
    return tuple(blur(sel, *zip(*halves)))


def solution(mesh):
    placed = (P("ifg", "row", None), P("ifg", "row", None), P())
    return jax.shard_map(
        on_device,
        mesh=mesh,
        in_specs=placed,
        out_specs=(P("ifg", "row", None), P("ifg", "row", None)),
        check_vma=False,
    )
```

```python
import functools
import math

import jax
import jax.numpy as jnp
import numpy as np
from jax import lax
from jax.experimental import pallas as pl
from jax.experimental.pallas import tpu as pltpu
from jax.sharding import PartitionSpec as P


PATCH = 64
HALF = PATCH // 2
RADIUS = 16
NDATES = 320
ITERS = 3

huber_threshold = 0.3
blur_sigma = 5.0

BF = jnp.bfloat16
F32 = jnp.float32


def mm(a, b):
    return jnp.dot(a, b, preferred_element_type=F32)


def split2(x):
    high = x.astype(BF)
    return high, (x - high.astype(F32)).astype(BF)


def split3(x):
    high = x.astype(BF)
    rest = x - high.astype(F32)
    mid = rest.astype(BF)
    return high, mid, (rest - mid.astype(F32)).astype(BF)


def mm3(a, b):
    ah, al = split2(a)
    bh, bl = split2(b)
    return mm(ah, bh) + (mm(ah, bl) + mm(al, bh))


def spectral_tables(local_rows):
    k = np.arange(PATCH)
    angles = ((k[:, None] * k[None, :]) % PATCH).astype(np.float32) * np.float32(
        2.0 * math.pi / PATCH
    )
    scaling = np.float32(1.0 / math.sqrt(PATCH))
    rounded = lambda v: np.asarray(v.astype(np.float32)).astype(BF).astype(np.float32)
    c = rounded(np.cos(angles) * scaling)
    s = rounded(np.sin(angles) * scaling)
    taper = (
        np.sin(np.float32(math.pi) * (k.astype(np.float32) + np.float32(0.5)) / PATCH) ** 2
    ).astype(np.float32)
    two = np.eye(2, dtype=np.float32)
    cc, ss = np.kron(two, c), np.kron(two, s)
    col_forward = np.block([[cc, -ss], [ss, cc]])
    col_inverse = np.block([[cc, ss], [-ss, cc]])
    extended = local_rows + PATCH
    starts = list(range(0, extended - PATCH + 1, HALF))
    count = len(starts)
    row_forward = np.zeros((2, count, PATCH, 2, extended), np.float32)
    row_inverse = np.zeros((2, extended, 2, count, PATCH), np.float32)
    for p, at in enumerate(starts):
        where = slice(at, at + PATCH)
        row_forward[0, p, :, 0, where] = c
        row_forward[0, p, :, 1, where] = s
        row_forward[1, p, :, 0, where] = -s
        row_forward[1, p, :, 1, where] = c
        tc, ts = taper[:, None] * c, taper[:, None] * s
        row_inverse[0, where, 0, p, :] = tc
        row_inverse[0, where, 1, p, :] = -ts
        row_inverse[1, where, 0, p, :] = ts
        row_inverse[1, where, 1, p, :] = tc
    row_forward = row_forward.reshape(2 * count * PATCH, 2 * extended)
    row_inverse = row_inverse[:, HALF : HALF + local_rows].reshape(
        2 * local_rows, 2 * count * PATCH
    )
    return (
        jnp.asarray(col_forward.astype(BF)),
        jnp.asarray(row_forward.astype(BF)),
        jnp.asarray(row_inverse.astype(BF)),
        jnp.asarray(col_inverse.astype(BF)),
        jnp.asarray(np.tile(taper, 4)[None, :]),
    )


def pick(sel, first, second, swapped_at, kept_at):
    zero = jnp.zeros_like(first)
    return jnp.where(sel[swapped_at] > 0, first, jnp.where(sel[kept_at] > 0, second, zero))


def filter_kernel(first, width, split, sel, re, im, one, two, *refs):
    if split:
        one_more, two_more, *refs = refs
    cf, rf, ri, ci, tp, out, pad_re, pad_im, even_re, even_im, odd_re, odd_im = refs
    group, rows, _ = re.shape
    extended = rows + PATCH
    window = width + 128
    start = 128 * first
    per = width // 128
    tiles = [(True, t) for t in range(per)] + [(False, t) for t in range(per + 1)]
    half = rf.shape[0] // 2

    @pl.when(pl.program_id(0) == 0)
    def _():
        pad_re[...] = jnp.zeros_like(pad_re)
        pad_im[...] = jnp.zeros_like(pad_im)

    def halo(part, i):
        p, q = one[part, i], two[part, i]
        if split:
            p = jnp.concatenate([p[:, start:], one_more[part, i]], axis=1)
            q = jnp.concatenate([q[:, start:], two_more[part, i]], axis=1)
        return pick(sel, p, q, 0, 1), pick(sel, p, q, 2, 3)

    def load(i, slot):
        made = []
        for part, own, pad in ((0, re, pad_re), (1, im, pad_im)):
            low, high = halo(part, i)
            x = jnp.concatenate([low, own[i, :, start : start + window], high], axis=0)
            pad[slot, :, HALF : HALF + window] = x
            made.append(x)
        return made

    def pair(step, carry):
        images = [load(2 * step + slot, slot) for slot in range(2)]
        members = [(slot, *tile) for tile in tiles for slot in range(2)]
        blocks = [members[n : n + 2] for n in range(0, len(members), 2)]

        def tile_of(slot, even, t):
            at = slice(start + 128 * t, start + 128 * t + 128)
            if even:
                return jnp.concatenate([x[:, at] for x in images[slot]], axis=1)
            return jnp.concatenate([pad_re[slot, :, at], pad_im[slot, :, at]], axis=1)

        def columns(n):
            stacked = jnp.concatenate([tile_of(*m) for m in blocks[n]], axis=0)
            y = mm(stacked, cf[...]).astype(BF)
            return jnp.concatenate(
                [
                    jnp.concatenate([y[:extended, :128], y[:extended, 128:]], axis=0),
                    jnp.concatenate([y[extended:, :128], y[extended:, 128:]], axis=0),
                ],
                axis=1,
            )

        def spectrum(y):
            z = mm(rf[...], y)
            z_re, z_im = z[:half], z[half:]
            gain = lax.rsqrt(lax.rsqrt(z_re * z_re + z_im * z_im + 1.0))
            return jnp.concatenate([(z_re * gain).astype(BF), (z_im * gain).astype(BF)], axis=0)

        def rows_back(q):
            u = mm(ri[...], q).astype(BF)
            return jnp.concatenate(
                [
                    jnp.concatenate([u[:rows, :128], u[rows:, :128]], axis=1),
                    jnp.concatenate([u[:rows, 128:], u[rows:, 128:]], axis=1),
                ],
                axis=0,
            )

        def columns_back(n, u):
            v = mm(u, ci[...]) * tp[...]
            for m, (slot, even, t) in enumerate(blocks[n]):
                piece = v[m * rows : (m + 1) * rows]
                at = slice(128 * t, 128 * t + 128)
                (even_re if even else odd_re)[slot, :, at] = piece[:, :128]
                (even_im if even else odd_im)[slot, :, at] = piece[:, 128:]

        count = len(blocks)
        y, q, u = {}, {}, {}
        for tick in range(count + 3):
            if tick < count:
                y[tick] = columns(tick)
            if 0 <= tick - 1 < count:
                q[tick - 1] = spectrum(y.pop(tick - 1))
            if 0 <= tick - 2 < count:
                u[tick - 2] = rows_back(q.pop(tick - 2))
            if 0 <= tick - 3 < count:
                columns_back(tick - 3, u.pop(tick - 3))
        for slot in range(2):
            f_re = even_re[slot] + odd_re[slot, :, HALF : HALF + width]
            f_im = even_im[slot] + odd_im[slot, :, HALF : HALF + width]
            out[2 * step + slot] = (f_im * lax.rsqrt(f_re * f_re + f_im * f_im + 1.0)).astype(BF)
        return carry

    lax.fori_loop(0, group // 2, pair, 0)


def filtered_sines(re, im, sel, halos, more, tables, at, count, first, width):
    rows, cols = re.shape[1:]
    group = 8
    extended = rows + PATCH
    skip = at // group
    whole = pl.BlockSpec((group, rows, cols), lambda i: (i + skip, 0, 0))
    edge = pl.BlockSpec((2, group, HALF, width + 128), lambda i: (0, i, 0, 0))
    rest = pl.BlockSpec((2, group, HALF, cols - width - 128), lambda i: (0, i + skip, 0, 0))
    fixed = [pl.BlockSpec(t.shape, lambda i: (0, 0)) for t in tables]
    return pl.pallas_call(
        functools.partial(filter_kernel, first, width, bool(more)),
        grid=(count // group,),
        in_specs=[pl.BlockSpec(memory_space=pltpu.SMEM), whole, whole, edge, edge]
        + [rest] * len(more)
        + fixed,
        out_specs=pl.BlockSpec((group, rows, width), lambda i: (i, 0, 0)),
        out_shape=jax.ShapeDtypeStruct((count, rows, width), BF),
        scratch_shapes=[pltpu.VMEM((2, extended, width + 256), BF)] * 2
        + [pltpu.VMEM((2, rows, width), F32)] * 2
        + [pltpu.VMEM((2, rows, width + 128), F32)] * 2,
        compiler_params=pltpu.CompilerParams(vmem_limit_bytes=32 << 20),
        cost_estimate=pl.CostEstimate(
            flops=count * width * 3000000, bytes_accessed=count * rows * cols * 4, transcendentals=0
        ),
        name="goldstein",
    )(sel, re, im, *halos, *more, *tables)


def inverse_kernel(steps, pairs, pairs_t, k_hi, k_lo, p_hi, p_lo):
    n = pairs.shape[0]
    dates = p_hi.shape[0]
    a, b = pairs[:, 0:1], pairs[:, 1:2]
    at, bt = pairs_t[0:1, :], pairs_t[1:2, :]
    one = lambda m: jnp.where(m, 1.0, 0.0)
    row = lax.broadcasted_iota(jnp.int32, (n, n), 0)
    col = lax.broadcasted_iota(jnp.int32, (n, n), 1)
    eye = one(row == col)
    matrix = one(a == at) + one(b == bt) - one(a == bt) - one(b == at) + eye
    exact = matrix.astype(BF)
    top = jnp.max(jnp.sum(jnp.abs(matrix), axis=1, keepdims=True), axis=0, keepdims=True)
    rho = (top - 1.0) / (top + 1.0)
    x = eye * (2.0 / (top + 1.0))

    def refine(_, carry):
        x, rho = carry
        xh, xm, xl = split3(x)
        residual = eye - (mm(exact, xh) + (mm(exact, xm) + mm(exact, xl)))
        scale = 2.0 / (2.0 - rho * rho)
        return (x + mm3(x, residual)) * scale, rho * rho / (2.0 - rho * rho)

    x, rho = lax.fori_loop(0, steps, refine, (x, rho))
    xh, xm, xl = split3(x)
    date = lax.broadcasted_iota(jnp.int32, (dates, n), 0)
    design_t = (one(date == bt) - one(date == at)).astype(BF)
    k_hi[...], k_lo[...] = split2(x)
    p_hi[...], p_lo[...] = split2(mm(design_t, xh) + (mm(design_t, xm) + mm(design_t, xl)))


def inverse_tables(date_pairs):
    n = date_pairs.shape[0]
    top, steps = 2.0 * n + 1.0, 0
    rho = (top - 1.0) / (top + 1.0)
    while rho > 1e-7:
        rho = rho * rho / (2.0 - rho * rho)
        steps += 1
    vmem = pl.BlockSpec(memory_space=pltpu.VMEM)
    return pl.pallas_call(
        functools.partial(inverse_kernel, steps),
        in_specs=[vmem, vmem],
        out_specs=[vmem] * 4,
        out_shape=[jax.ShapeDtypeStruct((n, n), BF)] * 2
        + [jax.ShapeDtypeStruct((NDATES, n), BF)] * 2,
        compiler_params=pltpu.CompilerParams(vmem_limit_bytes=40 << 20),
        cost_estimate=pl.CostEstimate(
            flops=steps * 6 * 4 * n**3, bytes_accessed=8 * n * n, transcendentals=0
        ),
        name="newton",
    )(date_pairs, date_pairs.T)


def invert_kernel(d_ref, k_hi, k_lo, p_hi, p_lo, out):
    parts, _, held, cols = d_ref.shape
    d = d_ref[:, 0].reshape(parts * held, cols).astype(F32)
    clip = lambda r: jnp.minimum(jnp.maximum(r, -huber_threshold), huber_threshold)

    def apply(high, low, v):
        v = v.astype(BF)
        return mm(high[...], v) + mm(low[...], v)

    total = clip(d)
    for _ in range(ITERS - 1):
        total = total + clip(d - total + apply(k_hi, k_lo, total))
    series = apply(p_hi, p_lo, total)
    out[:, 0] = series.reshape(parts, series.shape[0] // parts, cols).astype(out.dtype)


def invert(sines, tables):
    parts, strips, held, cols = sines.shape
    mine = NDATES // parts
    fixed = [pl.BlockSpec(t.shape, lambda i: (0, 0)) for t in tables]
    n = parts * held
    return pl.pallas_call(
        invert_kernel,
        grid=(strips,),
        in_specs=[pl.BlockSpec((parts, 1, held, cols), lambda i: (0, i, 0, 0))] + fixed,
        out_specs=pl.BlockSpec((parts, 1, mine, cols), lambda i: (0, i, 0, 0)),
        out_shape=jax.ShapeDtypeStruct((parts, strips, mine, cols), BF),
        compiler_params=pltpu.CompilerParams(vmem_limit_bytes=32 << 20),
        cost_estimate=pl.CostEstimate(
            flops=6 * strips * cols * n * (2 * n + NDATES),
            bytes_accessed=4 * strips * cols * n,
            transcendentals=0,
        ),
        name="huber",
    )(sines, *tables)


def gauss_matrix(size_out, size_in, offset):
    distance = np.arange(size_in)[None, :] - offset - np.arange(size_out)[:, None]
    kernel = np.exp(-0.5 * (distance.astype(np.float32) / np.float32(blur_sigma)) ** 2)
    return np.where(np.abs(distance) <= RADIUS, kernel, 0.0).astype(np.float32)


def blur_kernel(halves, sel, *refs):
    owns, ones, twos = refs[:halves], refs[halves : 2 * halves], refs[2 * halves : 3 * halves]
    rk, ck_hi, ck_lo, inv_row, inv_col, corrected, atmosphere = refs[3 * halves :]
    group, rows, _ = corrected.shape
    pieces = []
    own = []
    for i in range(group):
        own.append(jnp.concatenate([o[i] for o in owns], axis=1))
        one = jnp.concatenate([o[i] for o in ones], axis=1)
        two = jnp.concatenate([o[i] for o in twos], axis=1)
        extended = jnp.concatenate(
            [pick(sel, one, two, 0, 1), own[i], pick(sel, one, two, 2, 3)], axis=0
        )
        both = mm(rk[...], extended)
        pieces.append((both[:rows] + both[rows:]).astype(BF))
    stacked = jnp.concatenate(pieces, axis=0)
    smooth = mm(stacked, ck_hi[...]) + mm(stacked, ck_lo[...])
    for i in range(group):
        air = smooth[i * rows : (i + 1) * rows] * inv_row[...] * inv_col[...]
        atmosphere[i] = air
        corrected[i] = own[i].astype(F32) - air


def blur(sel, owns, ones, twos):
    dates, rows, _ = owns[0].shape
    cols = sum(o.shape[2] for o in owns)
    halves = len(owns)
    group = next(g for g in (8, 5, 4, 2, 1) if dates % g == 0)
    hi = lambda v: v.astype(BF)
    lo = lambda v: (v - v.astype(BF).astype(np.float32)).astype(BF)
    row_filter = gauss_matrix(rows, rows + 2 * RADIUS, RADIUS)
    col_filter = gauss_matrix(cols, cols, 0)
    row_tables = jnp.asarray(np.concatenate([hi(row_filter), lo(row_filter)], axis=0))
    source = lax.axis_index("row") * rows - RADIUS + jnp.arange(rows + 2 * RADIUS, dtype=jnp.int32)
    inside = (source >= 0) & (source < rows * lax.axis_size("row"))
    row_weight = jnp.sum(jnp.where(inside[None, :], jnp.asarray(row_filter), 0.0), axis=1)
    fixed = [
        row_tables,
        jnp.asarray(hi(col_filter)),
        jnp.asarray(lo(col_filter)),
        (1.0 / row_weight)[:, None],
        jnp.asarray(1.0 / col_filter.sum(axis=0, dtype=np.float32))[None, :],
    ]
    block = pl.BlockSpec((group, rows, cols), lambda i: (i, 0, 0))
    cut = lambda v: pl.BlockSpec((group,) + v.shape[1:], lambda i: (i, 0, 0))
    arrays = [*owns, *ones, *twos]
    return pl.pallas_call(
        functools.partial(blur_kernel, halves),
        grid=(dates // group,),
        in_specs=[pl.BlockSpec(memory_space=pltpu.SMEM)]
        + [cut(v) for v in arrays]
        + [pl.BlockSpec(t.shape, lambda i: (0, 0)) for t in fixed],
        out_specs=[block, block],
        out_shape=[jax.ShapeDtypeStruct((dates, rows, cols), F32)] * 2,
        compiler_params=pltpu.CompilerParams(vmem_limit_bytes=50 << 20),
        name="blur",
    )(sel, *arrays, *fixed)


def exchange(top, bottom):
    n = lax.axis_size("row")
    even = lax.axis_index("row") % 2 == 0
    received = []
    for first, mine in ((0, jnp.where(even, bottom, top)), (1, jnp.where(even, top, bottom))):
        partner = list(range(n))
        for i in range(first, n - 1, 2):
            partner[i], partner[i + 1] = i + 1, i
        received.append(lax.ppermute(mine, "row", list(enumerate(partner))))
    return received


def sources():
    n, at = lax.axis_size("row"), lax.axis_index("row")
    even = at % 2 == 0
    flags = [~even, even & (at > 0), even & (at < n - 1), ~even & (at < n - 1)]
    return jnp.stack(flags).astype(jnp.int32)


def on_device(ifg_real, ifg_imag, date_pairs):
    count, rows, cols = ifg_real.shape
    parts = lax.axis_size("ifg")
    strip = rows // parts
    width = cols // 2
    cut = width + 128
    tables = spectral_tables(rows)
    groups = [(0, 8), (8, count - 8)] if count > 8 else [(0, count)]
    halos = []
    for at, size in groups:
        joined = jnp.stack([v[at : at + size, :, :cut] for v in (ifg_real, ifg_imag)])
        halos.append(exchange(joined[:, :, :HALF], joined[:, :, rows - HALF :]))
    joined = jnp.stack([v[:, :, cut:] for v in (ifg_real, ifg_imag)])
    more = exchange(joined[:, :, :HALF], joined[:, :, rows - HALF :])
    sel = sources()
    solver = inverse_tables(date_pairs)
    gate, *solver = lax.optimization_barrier((sel, *solver))

    def sines_of(n, gate, first, extra):
        at, size = groups[n]
        return filtered_sines(
            ifg_real, ifg_imag, gate, halos[n], extra, tables, at, size, first, width
        )

    def send(pieces):
        sines = jnp.concatenate(pieces, axis=0) if len(pieces) > 1 else pieces[0]
        sines = sines.reshape(count, parts, strip, width).transpose(1, 2, 0, 3)
        return lax.all_to_all(sines, "ifg", split_axis=0, concat_axis=0, tiled=True)

    def give(series):
        return lax.all_to_all(series, "ifg", split_axis=0, concat_axis=0, tiled=True)

    def bordered(values):
        values = values.transpose(2, 0, 1, 3).reshape(NDATES // parts, rows, width)
        one, two = exchange(values[:, :RADIUS], values[:, rows - RADIUS :])
        return values, one, two

    skipped = width // 128 - 1
    left = send([sines_of(n, gate, 0, ()) for n in range(len(groups))])
    right = [sines_of(0, gate, skipped, more)]
    series = invert(left, solver)
    gate, series = lax.optimization_barrier((gate, series))
    out_left = give(series)
    right += [sines_of(n, gate, skipped, more) for n in range(1, len(groups))]
    *right, out_left = lax.optimization_barrier((*right, out_left))
    out_right = give(invert(send(right), solver))
    halves = [bordered(out_left), bordered(out_right)]
    return tuple(blur(sel, *zip(*halves)))


def solution(mesh):
    placed = (P("ifg", "row", None), P("ifg", "row", None), P())

    return jax.shard_map(
        on_device,
        mesh=mesh,
        in_specs=placed,
        out_specs=(P("ifg", "row", None), P("ifg", "row", None)),
        check_vma=False,
    )
```
